32 devices in a mesh: dp: 8 (over y, x, core), expert: 4 (over z).
Axes of the slice: x: 2, y: 2, z: 4, core: 2. Of those that a mesh axis runs over, the one named last changes fastest.
Arguments:
- grad_out: bfloat16 [4096, 2048], P(('dp', 'expert')), may hold values from -6 to 6
- probs: bfloat16 [4096, 2], P(('dp', 'expert')), may hold values from 0.099609375 to 1
- routes: int32 [4096, 2], P(('dp', 'expert')), may hold values from 0 to 3, all different within a row; in each aligned block of 128 rows (0 to 127, 128 to 255, ...) at most 80 rows name the same one
- hidden: bfloat16 [4, 2560, 7168], P('expert', None, 'dp'), may hold values from -0.119628906 to 0.119628906
- w_down: bfloat16 [4, 7168, 2048], P('expert', 'dp'), may hold values from -0.125 to 0.125
Outputs:
- grad_hidden: bfloat16 [4, 2560, 7168], P('expert', None, 'dp')
- grad_down: bfloat16 [4, 7168, 2048], P('expert', 'dp')
- grad_probs: float32 [4096, 2], P(('dp', 'expert'))
The draws below stay inside these ranges and needn't reach their ends.
Inputs may be any that keep to these rules, and one draw needn't show every extreme that they name: Within the 128 tokens of one device no expert is named by more than 80 routes; the 2 routes of a token name different experts; every expert is named somewhere.
All inputs are finite; a program needn't handle non-finite values.
Results may differ from the reference program's by a relative error of at most 0.0049.
Values may be sent and summed in bfloat16 or wider, within the bound.
A program may use at most 128 MiB of HBM per device.

```python
import math
import jax
import jax.numpy as jnp
import numpy as np
from jax import lax

D = 2048
FF = 7168
TOP = 2
TOK_DEV = 128
EXPERTS = 4
TOKENS = 4096
CAP = 80
SLOTS = 2560
N_DP = 8
N_EXPERT = 4


def shard_levels(stream_key, dims, split, low, top_value):
    def one(axis_at, blocks):
        heights = jax.random.uniform(jax.random.fold_in(jax.random.fold_in(stream_key, 6), axis_at), (blocks,), jnp.float32, low / len(split), top_value / len(split))
        return jnp.repeat(jnp.exp(heights), dims[axis_at] // blocks).reshape((-1,) + (1,) * (len(dims) - axis_at - 1))

    level = one(*split[0])
    for cut in split[1:]:
        level = level * one(*cut)
    return level


def deal_out(rng, own, number, rows, count, top, reach, lean):
    sequence = jax.random.permutation(rng, count)
    crowded, ordinary = shares(count, rows * top, reach, lean, True), shares(count, rows * top, reach, lean, False)
    places = jnp.arange(count)

    def named(lengths, offset_by):
        used = int((lengths > 0).sum())
        fixed = max(1, used // 4)
        moved = fixed + (places - fixed + offset_by * (used - fixed)) % max(1, count - fixed)
        return jnp.zeros((count,), jnp.int32).at[sequence[jnp.where(places < fixed, places, moved)]].set(jnp.asarray(lengths, jnp.int32))

    lengths = jnp.where(number % 4 == 0, named(crowded, number // 4), named(ordinary, number - number // 4 - 1))
    mixed = jax.random.permutation(jax.random.fold_in(own, 3), count)
    giver, sink = mixed[0:count // 2 * 2:2], mixed[1:count // 2 * 2:2]
    room = jnp.minimum(lengths[giver] - 1, reach - lengths[sink]) // 2
    room = jnp.where((giver == sequence[0]) | (sink == sequence[0]) | (lengths[sink] == 0), 0, jnp.maximum(room, 0))
    moved = jax.random.randint(jax.random.fold_in(own, 4), (count // 2,), 0, 1 << 20) % (room + 1)
    lengths = lengths.at[giver].add(-moved).at[sink].add(moved)
    members = jnp.searchsorted(jnp.cumsum(lengths), jnp.arange(rows * top), side="right").astype(jnp.int32)
    table = members.reshape(top, rows).T
    table = table[jax.random.permutation(jax.random.fold_in(own, 1), rows)]
    offset_by = jax.random.randint(jax.random.fold_in(own, 2), (rows, 1), 0, top)
    return jnp.take_along_axis(table, (jnp.arange(top)[None, :] + offset_by) % top, axis=1)


def shares(amount, total, bound, skew, full):
    weights = [(1 << 20) // math.isqrt(rank ** skew) + 1 for rank in range(1, amount + 1)]
    largest = bound if full else min(bound, max(-(-total // amount), total * weights[0] // sum(weights)))
    least = 1 if total - largest >= amount - 1 else 0
    holding, rest = [largest] + [least] * (amount - 1), total - largest - least * (amount - 1)
    while rest > 0:
        candidates = [i for i in range(1, amount) if holding[i] < largest] or [i for i in range(1, amount) if holding[i] < bound]
        pool, budget = sum([weights[i] for i in candidates]), rest
        for i in candidates:
            more = min(bound - holding[i], max(1, budget * weights[i] // pool), rest)
            holding[i] = holding[i] + more
            rest = rest - more
    return np.array(holding)


def gaussian(rng, shape, deviation, most, shards=(), held_as=jnp.bfloat16):
    values = deviation * jax.random.normal(rng, shape, jnp.float32)
    if shards:
        values = values * shard_levels(rng, shape, shards, -0.22, 0.18)
    return jnp.clip(values, -most, most).astype(held_as)


def setup_inputs(seed: int = 0) -> dict:
    splits = jax.random.split(jax.random.key(seed), 6)
    grad_out = gaussian(splits[0], (TOKENS, D), 1.0, 6.0, ((0, 32),))
    probs = jnp.clip(0.099609375 + 0.9003906 * jax.random.uniform(splits[1], (TOKENS, TOP), jnp.float32) ** shard_levels(splits[1], (TOKENS, TOP), ((0, 32),), -0.2, 0.2), 0.099609375, 1.0).astype(jnp.bfloat16)
    routes_keys = jax.random.split(jax.random.fold_in(splits[2], 1), TOKENS // TOK_DEV)
    routes_turns = jax.random.permutation(jax.random.fold_in(splits[2], 3), TOKENS // TOK_DEV)
    routes = jax.vmap(lambda own, number: deal_out(jax.random.fold_in(splits[2], 2), own, number, TOK_DEV, N_EXPERT, TOP, CAP, 1))(routes_keys, routes_turns).reshape((TOKENS, TOP))
    hidden = gaussian(splits[3], (EXPERTS, SLOTS, FF), 0.02, 0.119628906, ((0, 4), (2, 8)))
    w_down = gaussian(splits[4], (EXPERTS, FF, D), D ** -0.5, 0.125, ((0, 4), (1, 8)))
    return dict(grad_out=grad_out, probs=probs, routes=routes, hidden=hidden, w_down=w_down)


def expert_terms(operands):
    routed_rows, routed_weight, hidden_rows, weight_rows = operands
    weight_col = routed_weight.astype(jnp.float32)[:, None]
    scaled = (weight_col * routed_rows.astype(jnp.float32)).astype(jnp.bfloat16)
    back_hidden = jnp.dot(routed_rows, weight_rows.T, preferred_element_type=jnp.float32)
    grad_rows = (weight_col * back_hidden).astype(jnp.bfloat16)
    slot_probs = jnp.sum(hidden_rows.astype(jnp.float32) * back_hidden, axis=1)
    grad_weight = jnp.dot(hidden_rows.T, scaled, preferred_element_type=jnp.float32).astype(jnp.bfloat16)
    return grad_rows, grad_weight, slot_probs


def reference(grad_out, probs, routes, hidden, w_down):
    block_count = N_DP * N_EXPERT
    flattened = routes.reshape(block_count, TOK_DEV * TOP)
    expert_ids = jnp.arange(N_EXPERT, dtype=jnp.int32)
    one_hot = (flattened[:, :, None] == expert_ids[None, None, :]).astype(jnp.int32)
    ranking = jnp.cumsum(one_hot, axis=1) - 1
    within = jnp.sum(one_hot * ranking, axis=2)
    block_ids = jnp.arange(block_count, dtype=jnp.int32)[:, None]
    slot_index = (block_ids * CAP + within).reshape(-1).astype(jnp.int32)
    position = (routes.reshape(-1) * SLOTS + slot_index).astype(jnp.int32)
    token_of = jnp.repeat(jnp.arange(TOKENS, dtype=jnp.int32), TOP)
    routed = jnp.zeros((N_EXPERT * SLOTS, D), jnp.bfloat16).at[position].set(grad_out[token_of])
    routed_probs = jnp.zeros((N_EXPERT * SLOTS,), jnp.bfloat16).at[position].set(probs.reshape(-1))
    routed = routed.reshape(N_EXPERT, SLOTS, D)
    routed_probs = routed_probs.reshape(N_EXPERT, SLOTS)
    grad_hidden, grad_down, slot_probs = lax.map(expert_terms, (routed, routed_probs, hidden, w_down))
    grad_probs = slot_probs.reshape(-1)[position].reshape(TOKENS, TOP)
    return grad_hidden, grad_down, grad_probs
```

```python
import functools

import jax
import jax.numpy as jnp
from jax import lax
from jax.experimental import pallas as pl
from jax.experimental.pallas import tpu as pltpu
from jax.sharding import PartitionSpec as P

MESH = pl.DeviceIdType.MESH
LANES = 128
SUB = 8
F32 = jnp.float32
BF16 = jnp.bfloat16


def iota(shape, axis):
    return lax.broadcasted_iota(jnp.int32, shape, axis)


def as_row(column, lanes):
    shape = (column.shape[0], lanes)
    return jnp.sum(jnp.where(iota(shape, 0) == iota(shape, 1), column, 0), axis=0, keepdims=True)


def as_column(row, count):
    shape = (count, row.shape[1])
    return jnp.sum(jnp.where(iota(shape, 0) == iota(shape, 1), row, 0), axis=1, keepdims=True)


def flip(index, bits):
    bit = 1
    while bit <= bits:
        if bits & bit:
            index = index + bit * (1 - 2 * ((index // bit) % 2))
        bit *= 2
    return index


def pack_kernel(n_e, cap, x_ref, probs_ref, routes_ref, rows_ref, p_ref, dest_ref):
    tokens, top = routes_ref.shape
    routes = routes_ref[...]
    probs = probs_ref[...].astype(F32)
    route_rows = [as_row(routes[:, k : k + 1], tokens) for k in range(top)]
    prob_rows = [as_row(probs[:, k : k + 1], tokens) for k in range(top)]
    square = (tokens, tokens)
    before = iota(square, 0) < iota(square, 1)
    expert = iota((2 * SUB, tokens), 0)
    named = sum((expert == r).astype(F32) for r in route_rows)
    rank = jnp.dot(named.astype(BF16), before.astype(BF16), preferred_element_type=F32)
    rank = rank.astype(jnp.int32)
    x = x_ref[...]
    places = iota((cap, tokens), 0)
    dest = [jnp.zeros((1, tokens), jnp.int32) for _ in range(top)]
    for e in range(n_e):
        names = sum((r == e).astype(jnp.int32) for r in route_rows)
        weight = sum(jnp.where(r == e, p, 0.0) for r, p in zip(route_rows, prob_rows))
        rank_e = rank[e : e + 1, :]
        chosen = (places == rank_e) & (names > 0)
        rows_ref[e] = jnp.dot(chosen.astype(F32).astype(BF16), x, preferred_element_type=F32).astype(BF16)
        p_column = jnp.sum(jnp.where(chosen, weight, 0.0), axis=1, keepdims=True)
        p_ref[e] = jnp.broadcast_to(as_row(p_column, LANES), (SUB, LANES))
        for k in range(top):
            dest[k] = dest[k] + jnp.where(route_rows[k] == e, rank_e + e * LANES, 0)
    lane = iota((tokens, top), 1)
    out = jnp.zeros((tokens, top), jnp.int32)
    for k in range(top):
        out = jnp.where(lane == k, as_column(dest[k], tokens), out)
    dest_ref[...] = out


def main_kernel(
    n_e, n_d, cap,
    sent_ref, sentp_ref, dest_ref, hidden_ref, w_ref,
    gh_ref, gd_ref, gp_ref,
    rows, wv, wt, hbuf, gbuf, ht, scaled, acc, gdb,
    pz, pall, sbuf, sall, tot, tall,
    z_send, z_recv, b_send, b_recv, p_send, p_recv, q_send, q_recv,
    s_send, s_recv, t_send, t_recv, local, h_sem, g_sem, d_sem,
):
    d, z = lax.axis_index("dp"), lax.axis_index("expert")
    depth = w_ref.shape[1]
    half = depth // 2
    width = depth // d_sem.shape[0]
    ch = n_d // 2
    dc, dx, dy = flip(d, 1), flip(d, 2), flip(d, 4)
    dd = flip(d, 6)

    barrier = pltpu.get_barrier_semaphore()
    for k in range(1, n_e):
        pl.semaphore_signal(barrier, inc=1, device_id=(d, flip(z, k)), device_id_type=MESH)
    for j in range(1, n_d):
        pl.semaphore_signal(barrier, inc=1, device_id=(flip(d, j), z), device_id_type=MESH)
    w_copy = pltpu.make_async_copy(w_ref, wv, local.at[0])
    own_copy = pltpu.make_async_copy(sent_ref.at[z], rows.at[0, d], local.at[1])
    ownp_copy = pltpu.make_async_copy(sentp_ref.at[z], pz.at[0], local.at[2])
    own_copy.start()
    ownp_copy.start()
    w_copy.start()

    def h_copy(k):
        return pltpu.make_async_copy(hidden_ref.at[:, flip(z, k)], hbuf.at[k % 2], h_sem.at[k % 2])

    def g_copy(k):
        return pltpu.make_async_copy(gbuf.at[k % 2], gh_ref.at[:, flip(z, k)], g_sem.at[k % 2])

    h_copy(0).start()
    h_copy(1).start()
    pl.semaphore_wait(barrier, n_e + n_d - 2)

    def remote(src, dst, send, recv, to):
        return pltpu.make_async_remote_copy(
            src_ref=src, dst_ref=dst, send_sem=send, recv_sem=recv, device_id=to, device_id_type=MESH
        )

    def z_copy(k):
        to = flip(z, k)
        return remote(sent_ref.at[to], rows.at[k, d], z_send.at[k], z_recv.at[k], (d, to))

    def p_copy(k):
        to = flip(z, k)
        return remote(sentp_ref.at[to], pz.at[k], p_send.at[k], p_recv.at[k], (d, to))

    def q_copy(j):
        return remote(pz, pall.at[d], q_send.at[j], q_recv.at[j], (flip(d, j), z))

    def s_copy(j):
        to = flip(d, j)
        return remote(sbuf.at[to], sall.at[j], s_send.at[j], s_recv.at[j], (to, z))

    def t_copy(k):
        return remote(tot, tall.at[k], t_send.at[k], t_recv.at[k], (d, flip(z, k)))

    lo, hi = pl.ds(0, half), pl.ds(half, half)

    def b_copy(k, kind):
        whole = slice(None)
        src, cols, to = {
            0: (d, whole, dx),
            1: (d, whole, dy),
            2: (d, whole, dc),
            3: (dx, lo, dy),
            4: (dy, hi, dx),
            5: (dx, whole, dc),
            6: (dy, whole, dc),
            7: (dd, lo, dc),
            8: (dd, hi, dc),
        }[kind]
        part = rows.at[k, src] if cols is whole else rows.at[k, src, :, cols]
        return remote(part, part, b_send.at[k, kind], b_recv.at[k, kind], (to, z))

    def own_step(k):
        if k == 0:
            own_copy.wait()
        else:
            z_copy(k).wait_recv()
        for kind in (0, 1, 2):
            b_copy(k, kind).start()

    def side_step(k):
        b_copy(k, 0).wait_recv()
        b_copy(k, 3).start()
        b_copy(k, 5).start()
        b_copy(k, 1).wait_recv()
        b_copy(k, 4).start()
        b_copy(k, 6).start()

    def diagonal_step(k):
        b_copy(k, 3).wait_recv()
        b_copy(k, 7).start()
        b_copy(k, 4).wait_recv()
        b_copy(k, 8).start()

    def partner_step(k):
        for kind in (2, 5, 6, 7, 8):
            b_copy(k, kind).wait_recv()

    for k in range(1, n_e):
        p_copy(k).start()
    own_step(0)
    for k in range(1, n_e):
        z_copy(k).start()

    w_copy.wait()
    tile = 256 if depth % 256 == 0 else LANES

    @pl.loop(0, depth // tile)
    def _(i):
        at = pl.ds(pl.multiple_of(i * tile, tile), tile)
        wt[at, :] = wv[:, at].T

    ownp_copy.wait()
    for k in range(1, n_e):
        p_copy(k).wait_recv()
    for j in range(1, n_d):
        q_copy(j).start()
    own_p = pltpu.make_async_copy(pz, pall.at[d], local.at[3])
    own_p.start()
    own_step(1)
    side_step(0)
    own_p.wait()
    for j in range(1, n_d):
        q_copy(j).wait_recv()
    sbuf[...] = jnp.zeros_like(sbuf)

    for k in range(n_e):
        diagonal_step(k)
        partner_step(k)
        h_copy(k).wait()
        if k >= 2:
            g_copy(k - 2).wait()
        ht[...] = hbuf[k % 2].reshape(n_d * cap, -1).T

        @pl.loop(0, 2)
        def _(i):
            group = pl.ds(i * ch, ch)
            r = rows[k, group].reshape(ch * cap, depth)
            back = jnp.dot(r, wt[...], preferred_element_type=F32)
            p = jnp.concatenate([as_column(pall[i * ch + j, k, 0:1, :], cap) for j in range(ch)], axis=0)
            scaled[group] = (p * r.astype(F32)).astype(BF16).reshape(ch, cap, depth)
            gbuf[k % 2, group] = (p * back).astype(BF16).reshape(ch, cap, -1)
            h = hbuf[k % 2, group].reshape(ch * cap, -1).astype(F32)
            slot = jnp.sum(h * back, axis=1, keepdims=True)
            for j in range(ch):
                sbuf[i * ch + j, k : k + 1, :] = as_row(slot[j * cap : (j + 1) * cap], LANES)

        g_copy(k).start()
        if k + 2 < n_e:
            own_step(k + 2)
        if k + 1 < n_e:
            side_step(k + 1)
        else:
            for j in range(1, n_d):
                s_copy(j).start()

        @pl.loop(0, depth // width)
        def _(i):
            at = pl.ds(pl.multiple_of(i * width, width), width)
            part = jnp.dot(
                ht[...], scaled[:, :, at].reshape(n_d * cap, width), preferred_element_type=F32
            )
            if k > 0:
                part = acc[:, at] + part
            if k < n_e - 1:
                acc[:, at] = part
            else:
                gdb[:, at] = part.astype(BF16)
                pltpu.make_async_copy(gdb.at[:, at], gd_ref.at[:, at], d_sem.at[i]).start()

        if k + 2 < n_e:
            h_copy(k + 2).start()

    total = sbuf[d]
    for j in range(1, n_d):
        s_copy(j).wait_recv()
        total = total + sall[j]
    tot[...] = total
    for k in range(1, n_e):
        t_copy(k).start()
    tokens, top = dest_ref.shape
    lane = iota((tokens, top), 1)
    lanes = iota((tokens, LANES), 1)
    result = jnp.zeros((tokens, top), F32)
    for k in range(n_e):
        if k > 0:
            t_copy(k).wait_recv()
            row = tall[k][k : k + 1, :]
        else:
            row = total[0:1, :]
        base = flip(z, k) * LANES
        for t in range(top):
            hit = dest_ref[:, t : t + 1] == base + lanes
            value = jnp.sum(jnp.where(hit, row, 0.0), axis=1, keepdims=True)
            result = result + jnp.where(lane == t, value, 0.0)
    gp_ref[...] = result

    for k in range(1, n_e):
        z_copy(k).wait_send()
        p_copy(k).wait_send()
        t_copy(k).wait_send()
    for j in range(1, n_d):
        q_copy(j).wait_send()
        s_copy(j).wait_send()
    for k in range(n_e):
        for kind in range(9):
            b_copy(k, kind).wait_send()
    for k in range(max(0, n_e - 2), n_e):
        g_copy(k).wait()

    @pl.loop(0, depth // width)
    def _(i):
        at = pl.ds(pl.multiple_of(i * width, width), width)
        pltpu.make_async_copy(gdb.at[:, at], gd_ref.at[:, at], d_sem.at[i]).wait()


def on_device(grad_out, probs, routes, hidden, w_down):
    n_e, n_d = lax.axis_size("expert"), lax.axis_size("dp")
    tokens, top = routes.shape
    cap = tokens * top * 5 // (4 * n_e)
    depth = grad_out.shape[1]
    units = hidden.shape[2]
    slots = n_d * cap
    vmem = pl.BlockSpec(memory_space=pltpu.VMEM)
    hbm = pl.BlockSpec(memory_space=pl.ANY)
    rows, p, dest = pl.pallas_call(
        functools.partial(pack_kernel, n_e, cap),
        out_shape=(
            jax.ShapeDtypeStruct((n_e, cap, depth), BF16),
            jax.ShapeDtypeStruct((n_e, SUB, LANES), F32),
            jax.ShapeDtypeStruct((tokens, top), jnp.int32),
        ),
        in_specs=[vmem] * 3,
        out_specs=(vmem, vmem, vmem),
        name="pack",
    )(grad_out, probs, routes)
    dma = pltpu.SemaphoreType.DMA
    chunks = max(1, depth // 256)
    gh, gd, gp = pl.pallas_call(
        functools.partial(main_kernel, n_e, n_d, cap),
        out_shape=(
            jax.ShapeDtypeStruct((n_d, n_e, cap, units), BF16),
            jax.ShapeDtypeStruct((units, depth), BF16),
            jax.ShapeDtypeStruct((tokens, top), F32),
        ),
        in_specs=[hbm, hbm, vmem, hbm, hbm],
        out_specs=(hbm, hbm, vmem),
        scratch_shapes=[
            pltpu.VMEM((n_e, n_d, cap, depth), BF16),
            pltpu.VMEM((units, depth), BF16),
            pltpu.VMEM((depth, units), BF16),
            pltpu.VMEM((2, n_d, cap, units), BF16),
            pltpu.VMEM((2, n_d, cap, units), BF16),
            pltpu.VMEM((units, slots), BF16),
            pltpu.VMEM((n_d, cap, depth), BF16),
            pltpu.VMEM((units, depth), F32),
            pltpu.VMEM((units, depth), BF16),
            pltpu.VMEM((n_e, SUB, LANES), F32),
            pltpu.VMEM((n_d, n_e, SUB, LANES), F32),
            pltpu.VMEM((n_d, SUB, LANES), F32),
            pltpu.VMEM((n_d, SUB, LANES), F32),
            pltpu.VMEM((SUB, LANES), F32),
            pltpu.VMEM((n_e, SUB, LANES), F32),
            dma((n_e,)), dma((n_e,)),
            dma((n_e, 9)), dma((n_e, 9)),
            dma((n_e,)), dma((n_e,)),
            dma((n_d,)), dma((n_d,)),
            dma((n_d,)), dma((n_d,)),
            dma((n_e,)), dma((n_e,)),
            dma((4,)), dma((2,)), dma((2,)), dma((chunks,)),
        ],
        compiler_params=pltpu.CompilerParams(
            collective_id=0, has_side_effects=True, vmem_limit_bytes=62 * 1024 * 1024
        ),
        name="expert_back",
    )(rows, p, dest, hidden[0].reshape(n_d, n_e, cap, units), w_down[0])
    return gh.reshape(1, n_d * n_e * cap, units), gd[None], gp


def solution(mesh):
    in_specs = (
        P(("dp", "expert"), None),
        P(("dp", "expert"), None),
        P(("dp", "expert"), None),
        P("expert", None, "dp"),
        P("expert", "dp", None),
    )
    out_specs = (P("expert", None, "dp"), P("expert", "dp", None), P(("dp", "expert"), None))
    return jax.shard_map(
        on_device, mesh=mesh, in_specs=in_specs, out_specs=out_specs, check_vma=False
    )
```

```python
import functools

import jax
import jax.numpy as jnp
from jax import lax
from jax.experimental import pallas as pl
from jax.experimental.pallas import tpu as pltpu
from jax.sharding import PartitionSpec as P

MESH = pl.DeviceIdType.MESH
LANES = 128
SUB = 8
F32 = jnp.float32
BF16 = jnp.bfloat16


def iota(shape, axis):
    return lax.broadcasted_iota(jnp.int32, shape, axis)


def as_row(column, lanes):
    shape = (column.shape[0], lanes)
    return jnp.sum(jnp.where(iota(shape, 0) == iota(shape, 1), column, 0), axis=0, keepdims=True)


def as_column(row, count):
    shape = (count, row.shape[1])
    return jnp.sum(jnp.where(iota(shape, 0) == iota(shape, 1), row, 0), axis=1, keepdims=True)


def flip(index, bits):
    bit = 1
    while bit <= bits:
        if bits & bit:
            index = index + bit * (1 - 2 * ((index // bit) % 2))
        bit *= 2
    return index


def pack_kernel(n_e, cap, x_ref, probs_ref, routes_ref, rows_ref, p_ref, dest_ref):
    top, tokens = routes_ref.shape
    probs = probs_ref[...].astype(F32)
    route_rows = [routes_ref[k : k + 1, :] for k in range(top)]
    prob_rows = [probs[k : k + 1, :] for k in range(top)]
    square = (tokens, tokens)
    before = iota(square, 0) < iota(square, 1)
    expert = iota((2 * SUB, tokens), 0)
    named = sum((expert == r).astype(F32) for r in route_rows)
    rank = jnp.dot(named.astype(BF16), before.astype(BF16), preferred_element_type=F32)
    rank = rank.astype(jnp.int32)
    x = x_ref[...]
    places = iota((cap, tokens), 0)
    dest = [jnp.zeros((1, tokens), jnp.int32) for _ in range(top)]
    for e in range(n_e):
        names = sum((r == e).astype(jnp.int32) for r in route_rows)
        weight = sum(jnp.where(r == e, p, 0.0) for r, p in zip(route_rows, prob_rows))
        rank_e = rank[e : e + 1, :]
        chosen = (places == rank_e) & (names > 0)
        rows_ref[e] = jnp.dot(chosen.astype(F32).astype(BF16), x, preferred_element_type=F32).astype(BF16)
        p_column = jnp.sum(jnp.where(chosen, weight, 0.0), axis=1, keepdims=True)
        p_ref[e] = jnp.broadcast_to(as_row(p_column, LANES), (SUB, LANES))
        for k in range(top):
            dest[k] = dest[k] + jnp.where(route_rows[k] == e, rank_e + e * LANES, 0)
    for k in range(top):
        dest_ref[k : k + 1, :] = dest[k]


def main_kernel(
    n_e, n_d, cap,
    sent_ref, sentp_ref, dest_ref, hidden_ref, w_ref,
    gh_ref, gd_ref, gp_ref,
    rows, wv, wt, hbuf, gbuf, ht, ht_last, scaled, acc, gdb,
    pz, pall, sbuf, sall, tot, tall,
    z_send, z_recv, b_send, b_recv, p_send, p_recv, q_send, q_recv,
    s_send, s_recv, t_send, t_recv, local, h_sem, g_sem, d_sem,
):
    d, z = lax.axis_index("dp"), lax.axis_index("expert")
    depth = w_ref.shape[1]
    half = depth // 2
    width = depth // d_sem.shape[0]
    dc, dx, dy = flip(d, 1), flip(d, 2), flip(d, 4)
    dd = flip(d, 6)

    barrier = pltpu.get_barrier_semaphore()
    for k in range(1, n_e):
        pl.semaphore_signal(barrier, inc=1, device_id=(d, flip(z, k)), device_id_type=MESH)
    for j in range(1, n_d):
        pl.semaphore_signal(barrier, inc=1, device_id=(flip(d, j), z), device_id_type=MESH)
    w_copy = pltpu.make_async_copy(w_ref, wv, local.at[0])
    own_copy = pltpu.make_async_copy(sent_ref.at[z], rows.at[0, d], local.at[1])
    ownp_copy = pltpu.make_async_copy(sentp_ref.at[z], pz.at[0], local.at[2])
    own_copy.start()
    ownp_copy.start()
    w_copy.start()

    groups = n_d // 2

    def pair(g):
        return 2 * flip(d // 2, g)

    class Parts:
        def __init__(self, parts):
            self.parts = parts

        def start(self):
            for part in self.parts:
                part.start()

        def wait(self):
            for part in self.parts:
                part.wait()

    def h_copy(k):
        return Parts([
            pltpu.make_async_copy(
                hidden_ref.at[pl.ds(pair(g), 2), flip(z, k)], hbuf.at[k % 2, pl.ds(2 * g, 2)], h_sem.at[k % 2, g]
            )
            for g in range(groups)
        ])

    def g_copy(k, gs=range(n_d // 2)):
        return Parts([
            pltpu.make_async_copy(
                gbuf.at[k % 2, pl.ds(2 * g, 2)], gh_ref.at[pl.ds(pair(g), 2), flip(z, k)], g_sem.at[k % 2, g]
            )
            for g in gs
        ])

    h_copy(0).start()
    h_copy(1).start()
    pl.semaphore_wait(barrier, n_e + n_d - 2)

    def remote(src, dst, send, recv, to):
        return pltpu.make_async_remote_copy(
            src_ref=src, dst_ref=dst, send_sem=send, recv_sem=recv, device_id=to, device_id_type=MESH
        )

    def z_copy(k):
        to = flip(z, k)
        return remote(sent_ref.at[to], rows.at[k, d], z_send.at[k], z_recv.at[k], (d, to))

    def p_copy(k):
        to = flip(z, k)
        return remote(sentp_ref.at[to], pz.at[k], p_send.at[k], p_recv.at[k], (d, to))

    def q_copy(j):
        return remote(pz, pall.at[d], q_send.at[j], q_recv.at[j], (flip(d, j), z))

    def s_copy(j):
        to = flip(d, j)
        return remote(sbuf.at[to], sall.at[j], s_send.at[j], s_recv.at[j], (to, z))

    def t_copy(k):
        return remote(tot, tall.at[k], t_send.at[k], t_recv.at[k], (d, flip(z, k)))

    lo, hi = pl.ds(0, half), pl.ds(half, half)

    def b_copy(k, kind):
        whole = slice(None)
        src, cols, to = {
            0: (d, whole, dx),
            1: (d, whole, dy),
            2: (d, whole, dc),
            3: (dx, lo, dy),
            4: (dy, hi, dx),
            5: (dx, whole, dc),
            6: (dy, whole, dc),
            7: (dd, lo, dc),
            8: (dd, hi, dc),
        }[kind]
        part = rows.at[k, src] if cols is whole else rows.at[k, src, :, cols]
        return remote(part, part, b_send.at[k, kind], b_recv.at[k, kind], (to, z))

    def own_step(k):
        if k == 0:
            own_copy.wait()
        else:
            z_copy(k).wait_recv()
        for kind in (0, 1, 2):
            b_copy(k, kind).start()

    def side_step(k):
        b_copy(k, 0).wait_recv()
        b_copy(k, 3).start()
        b_copy(k, 5).start()
        b_copy(k, 1).wait_recv()
        b_copy(k, 4).start()
        b_copy(k, 6).start()

    def diagonal_step(k):
        b_copy(k, 3).wait_recv()
        b_copy(k, 7).start()
        b_copy(k, 4).wait_recv()
        b_copy(k, 8).start()

    def partner_step(k, kinds):
        for kind in kinds:
            b_copy(k, kind).wait_recv()

    for k in range(1, n_e):
        z_copy(k).start()
        p_copy(k).start()
    own_step(0)

    w_copy.wait()
    tile = 256 if depth % 256 == 0 else LANES

    @pl.loop(0, depth // tile)
    def _(i):
        at = pl.ds(pl.multiple_of(i * tile, tile), tile)
        wt[at, :] = wv[:, at].T

    ownp_copy.wait()
    for k in range(1, n_e):
        p_copy(k).wait_recv()
    for j in range(1, n_d):
        q_copy(j).start()
    own_p = pltpu.make_async_copy(pz, pall.at[d], local.at[3])
    own_p.start()
    sbuf[...] = jnp.zeros_like(sbuf)
    own_p.wait()
    for j in range(1, n_d):
        q_copy(j).wait_recv()

    def back_step(k, gs):
        first, count = 2 * gs[0], 2 * len(gs)
        members = [pair(g) + c for g in gs for c in range(2)]
        r = jnp.concatenate([rows[k, m] for m in members], axis=0)
        back = jnp.dot(r, wt[...], preferred_element_type=F32)
        p = jnp.concatenate([as_column(pall[m, k, 0:1, :], cap) for m in members], axis=0)
        at = pl.ds(first, count)
        scaled[at] = (p * r.astype(F32)).astype(BF16).reshape(count, cap, depth)
        gbuf[k % 2, at] = (p * back).astype(BF16).reshape(count, cap, -1)
        h = hbuf[k % 2, at].reshape(count * cap, -1).astype(F32)
        slot = jnp.sum(h * back, axis=1, keepdims=True)
        for j, m in enumerate(members):
            sbuf[m, k : k + 1, :] = as_row(slot[j * cap : (j + 1) * cap], LANES)
        g_copy(k, gs).start()

    def weight_step(k, first, count, turned, add, final, start=0, stop=depth // width):
        @pl.loop(start, stop)
        def _(i):
            at = pl.ds(pl.multiple_of(i * width, width), width)
            part = jnp.dot(
                turned[:, 0 : count * cap],
                scaled[first : first + count, :, at].reshape(count * cap, width),
                preferred_element_type=F32,
            )
            if add:
                part = acc[:, at] + part
            if final:
                gdb[:, at] = part.astype(BF16)
                pltpu.make_async_copy(gdb.at[:, at], gd_ref.at[:, at], d_sem.at[i]).start()
            else:
                acc[:, at] = part

    for k in range(n_e):
        last = k == n_e - 1
        h_copy(k).wait()
        if k >= 2:
            g_copy(k - 2).wait()
        if k == 0:
            partner_step(0, (2,))
            back_step(0, (0,))
            own_step(1)
            side_step(0)
            partner_step(0, (5,))
            back_step(0, (1,))
        else:
            partner_step(k, (2, 5))
            back_step(k, (0, 1))
        diagonal_step(k)
        if k + 2 < n_e:
            own_step(k + 2)
        partner_step(k, (6,))
        if not last:
            ht[...] = hbuf[k % 2].reshape(n_d * cap, -1).T
            partner_step(k, (7, 8))
            back_step(k, (2, 3))
            side_step(k + 1)
            weight_step(k, 0, n_d, ht, k > 0, False)
            if k + 2 < n_e:
                h_copy(k + 2).start()
        else:
            back_step(k, (2,))
            most = n_d - 2
            ht[:, 0 : most * cap] = hbuf[k % 2, 0:most].reshape(most * cap, -1).T
            ht_last[...] = hbuf[k % 2, most:n_d].reshape(2 * cap, -1).T
            weight_step(k, 0, most, ht, k > 0, False)
            partner_step(k, (7, 8))
            back_step(k, (3,))
            weight_step(k, most, 2, ht_last, True, True, 0, 1)
            for j in range(1, n_d):
                s_copy(j).start()
            weight_step(k, most, 2, ht_last, True, True, 1)

    total = sbuf[d]
    for j in range(1, n_d):
        s_copy(j).wait_recv()
        total = total + sall[j]
    tot[...] = total
    for k in range(1, n_e):
        t_copy(k).start()
    top, tokens = dest_ref.shape
    lanes = iota((LANES, tokens), 0)
    result = [jnp.zeros((1, tokens), F32) for _ in range(top)]
    for k in range(n_e):
        if k > 0:
            t_copy(k).wait_recv()
            row = tall[k][k : k + 1, :]
        else:
            row = total[0:1, :]
        column = as_column(row, LANES)
        base = flip(z, k) * LANES
        for t in range(top):
            hit = dest_ref[t : t + 1, :] == base + lanes
            result[t] = result[t] + jnp.sum(jnp.where(hit, column, 0.0), axis=0, keepdims=True)
    for t in range(top):
        gp_ref[t : t + 1, :] = result[t]

    for k in range(1, n_e):
        z_copy(k).wait_send()
        p_copy(k).wait_send()
        t_copy(k).wait_send()
    for j in range(1, n_d):
        q_copy(j).wait_send()
        s_copy(j).wait_send()
    for k in range(n_e):
        for kind in range(9):
            b_copy(k, kind).wait_send()
    for k in range(max(0, n_e - 2), n_e):
        g_copy(k).wait()

    @pl.loop(0, depth // width)
    def _(i):
        at = pl.ds(pl.multiple_of(i * width, width), width)
        pltpu.make_async_copy(gdb.at[:, at], gd_ref.at[:, at], d_sem.at[i]).wait()


def on_device(grad_out, probs, routes, hidden, w_down):
    n_e, n_d = lax.axis_size("expert"), lax.axis_size("dp")
    tokens, top = routes.shape
    cap = tokens * top * 5 // (4 * n_e)
    depth = grad_out.shape[1]
    units = hidden.shape[2]
    slots = n_d * cap
    vmem = pl.BlockSpec(memory_space=pltpu.VMEM)
    hbm = pl.BlockSpec(memory_space=pl.ANY)
    rows, p, dest = pl.pallas_call(
        functools.partial(pack_kernel, n_e, cap),
        out_shape=(
            jax.ShapeDtypeStruct((n_e, cap, depth), BF16),
            jax.ShapeDtypeStruct((n_e, SUB, LANES), F32),
            jax.ShapeDtypeStruct((top, tokens), jnp.int32),
        ),
        in_specs=[vmem] * 3,
        out_specs=(vmem, vmem, vmem),
        name="pack",
    )(grad_out, probs.T, routes.T)
    dma = pltpu.SemaphoreType.DMA
    chunks = max(1, depth // 256)
    gh, gd, gp = pl.pallas_call(
        functools.partial(main_kernel, n_e, n_d, cap),
        out_shape=(
            jax.ShapeDtypeStruct((n_d, n_e, cap, units), BF16),
            jax.ShapeDtypeStruct((units, depth), BF16),
            jax.ShapeDtypeStruct((top, tokens), F32),
        ),
        in_specs=[hbm, hbm, vmem, hbm, hbm],
        out_specs=(hbm, hbm, vmem),
        scratch_shapes=[
            pltpu.VMEM((n_e, n_d, cap, depth), BF16),
            pltpu.VMEM((units, depth), BF16),
            pltpu.VMEM((depth, units), BF16),
            pltpu.VMEM((2, n_d, cap, units), BF16),
            pltpu.VMEM((2, n_d, cap, units), BF16),
            pltpu.VMEM((units, slots), BF16),
            pltpu.VMEM((units, 2 * cap), BF16),
            pltpu.VMEM((n_d, cap, depth), BF16),
            pltpu.VMEM((units, depth), F32),
            pltpu.VMEM((units, depth), BF16),
            pltpu.VMEM((n_e, SUB, LANES), F32),
            pltpu.VMEM((n_d, n_e, SUB, LANES), F32),
            pltpu.VMEM((n_d, SUB, LANES), F32),
            pltpu.VMEM((n_d, SUB, LANES), F32),
            pltpu.VMEM((SUB, LANES), F32),
            pltpu.VMEM((n_e, SUB, LANES), F32),
            dma((n_e,)), dma((n_e,)),
            dma((n_e, 9)), dma((n_e, 9)),
            dma((n_e,)), dma((n_e,)),
            dma((n_d,)), dma((n_d,)),
            dma((n_d,)), dma((n_d,)),
            dma((n_e,)), dma((n_e,)),
            dma((4,)), dma((2, n_d // 2)), dma((2, n_d // 2)), dma((chunks,)),
        ],
        compiler_params=pltpu.CompilerParams(
            collective_id=0, has_side_effects=True, vmem_limit_bytes=62 * 1024 * 1024
        ),
        name="expert_back",
    )(rows, p, dest, hidden[0].reshape(n_d, n_e, cap, units), w_down[0])
    return gh.reshape(1, n_d * n_e * cap, units), gd[None], gp.T


def solution(mesh):
    in_specs = (
        P(("dp", "expert"), None),
        P(("dp", "expert"), None),
        P(("dp", "expert"), None),
        P("expert", None, "dp"),
        P("expert", "dp", None),
    )
    out_specs = (P("expert", None, "dp"), P("expert", "dp", None), P(("dp", "expert"), None))
    return jax.shard_map(
        on_device, mesh=mesh, in_specs=in_specs, out_specs=out_specs, check_vma=False
    )
```

```python
import functools

import jax
import jax.numpy as jnp
from jax import lax
from jax.experimental import pallas as pl
from jax.experimental.pallas import tpu as pltpu
from jax.sharding import PartitionSpec as P

MESH = pl.DeviceIdType.MESH
LANES = 128
SUB = 8
F32 = jnp.float32
BF16 = jnp.bfloat16


def iota(shape, axis):
    return lax.broadcasted_iota(jnp.int32, shape, axis)


def as_row(column, lanes):
    shape = (column.shape[0], lanes)
    return jnp.sum(jnp.where(iota(shape, 0) == iota(shape, 1), column, 0), axis=0, keepdims=True)


def as_column(row, count):
    shape = (count, row.shape[1])
    return jnp.sum(jnp.where(iota(shape, 0) == iota(shape, 1), row, 0), axis=1, keepdims=True)


def flip(index, bits):
    bit = 1
    while bit <= bits:
        if bits & bit:
            index = index + bit * (1 - 2 * ((index // bit) % 2))
        bit *= 2
    return index


def pack_kernel(n_e, cap, x_ref, probs_ref, routes_ref, rows_ref, p_ref, dest_ref):
    top, tokens = routes_ref.shape
    probs = probs_ref[...].astype(F32)
    route_rows = [routes_ref[k : k + 1, :] for k in range(top)]
    prob_rows = [probs[k : k + 1, :] for k in range(top)]
    square = (tokens, tokens)
    before = iota(square, 0) < iota(square, 1)
    expert = iota((2 * SUB, tokens), 0)
    named = sum((expert == r).astype(F32) for r in route_rows)
    rank = jnp.dot(named.astype(BF16), before.astype(BF16), preferred_element_type=F32)
    rank = rank.astype(jnp.int32)
    x = x_ref[...]
    places = iota((cap, tokens), 0)
    dest = [jnp.zeros((1, tokens), jnp.int32) for _ in range(top)]
    for e in range(n_e):
        names = sum((r == e).astype(jnp.int32) for r in route_rows)
        weight = sum(jnp.where(r == e, p, 0.0) for r, p in zip(route_rows, prob_rows))
        rank_e = rank[e : e + 1, :]
        chosen = (places == rank_e) & (names > 0)
        rows_ref[e] = jnp.dot(chosen.astype(F32).astype(BF16), x, preferred_element_type=F32).astype(BF16)
        p_column = jnp.sum(jnp.where(chosen, weight, 0.0), axis=1, keepdims=True)
        p_ref[e] = jnp.broadcast_to(as_row(p_column, LANES), (SUB, LANES))
        for k in range(top):
            dest[k] = dest[k] + jnp.where(route_rows[k] == e, rank_e + e * LANES, 0)
    for k in range(top):
        dest_ref[k : k + 1, :] = dest[k]


def main_kernel(
    n_e, n_d, cap,
    sent_ref, sentp_ref, dest_ref, hidden_ref, w_ref,
    gh_ref, gd_ref, gp_ref,
    rows, wv, wt, hbuf, gbuf, ht, ht_last, scaled, acc, gdb,
    pz, pall, sbuf, sall, tot, tall,
    z_send, z_recv, b_send, b_recv, p_send, p_recv, q_send, q_recv,
    s_send, s_recv, t_send, t_recv, local, h_sem, g_sem, d_sem,
):
    d, z = lax.axis_index("dp"), lax.axis_index("expert")
    depth = w_ref.shape[1]
    half = depth // 2
    width = depth // d_sem.shape[0]
    dc, dx, dy = flip(d, 1), flip(d, 2), flip(d, 4)
    dd = flip(d, 6)

    barrier = pltpu.get_barrier_semaphore()
    for k in range(1, n_e):
        pl.semaphore_signal(barrier, inc=1, device_id=(d, flip(z, k)), device_id_type=MESH)
    for j in range(1, n_d):
        pl.semaphore_signal(barrier, inc=1, device_id=(flip(d, j), z), device_id_type=MESH)
    w_copy = pltpu.make_async_copy(w_ref, wv, local.at[0])
    own_copy = pltpu.make_async_copy(sent_ref.at[z], rows.at[0, d], local.at[1])
    ownp_copy = pltpu.make_async_copy(sentp_ref.at[z], pz.at[0], local.at[2])
    own_copy.start()
    ownp_copy.start()
    w_copy.start()

    groups = n_d // 2

    def pair(g):
        return 2 * flip(d // 2, g)

    class Parts:
        def __init__(self, parts):
            self.parts = parts

        def start(self):
            for part in self.parts:
                part.start()

        def wait(self):
            for part in self.parts:
                part.wait()

    def h_copy(k):
        return Parts([
            pltpu.make_async_copy(
                hidden_ref.at[pl.ds(pair(g), 2), flip(z, k)], hbuf.at[k % 2, pl.ds(2 * g, 2)], h_sem.at[k % 2, g]
            )
            for g in range(groups)
        ])

    def g_copy(k, gs=range(n_d // 2)):
        return Parts([
            pltpu.make_async_copy(
                gbuf.at[k % 2, pl.ds(2 * g, 2)], gh_ref.at[pl.ds(pair(g), 2), flip(z, k)], g_sem.at[k % 2, g]
            )
            for g in gs
        ])

    h_copy(0).start()
    h_copy(1).start()
    pl.semaphore_wait(barrier, n_e + n_d - 2)

    def remote(src, dst, send, recv, to):
        return pltpu.make_async_remote_copy(
            src_ref=src, dst_ref=dst, send_sem=send, recv_sem=recv, device_id=to, device_id_type=MESH
        )

    def z_copy(k):
        to = flip(z, k)
        return remote(sent_ref.at[to], rows.at[k, d], z_send.at[k], z_recv.at[k], (d, to))

    def p_copy(k):
        to = flip(z, k)
        return remote(sentp_ref.at[to], pz.at[k], p_send.at[k], p_recv.at[k], (d, to))

    def q_copy(j):
        return remote(pz, pall.at[d], q_send.at[j], q_recv.at[j], (flip(d, j), z))

    def s_copy(j):
        to = flip(d, j)
        return remote(sbuf.at[to], sall.at[j], s_send.at[j], s_recv.at[j], (to, z))

    def t_copy(k):
        return remote(tot, tall.at[k], t_send.at[k], t_recv.at[k], (d, flip(z, k)))

    lo, hi = pl.ds(0, half), pl.ds(half, half)

    def b_copy(k, kind):
        whole = slice(None)
        src, cols, to = {
            0: (d, whole, dx),
            1: (d, whole, dy),
            2: (d, whole, dc),
            3: (dx, lo, dy),
            4: (dy, hi, dx),
            5: (dx, whole, dc),
            6: (dy, whole, dc),
            7: (dd, lo, dc),
            8: (dd, hi, dc),
        }[kind]
        part = rows.at[k, src] if cols is whole else rows.at[k, src, :, cols]
        return remote(part, part, b_send.at[k, kind], b_recv.at[k, kind], (to, z))

    def own_step(k):
        if k == 0:
            own_copy.wait()
        else:
            z_copy(k).wait_recv()
        for kind in (0, 1, 2):
            b_copy(k, kind).start()

    def side_step(k):
        b_copy(k, 0).wait_recv()
        b_copy(k, 3).start()
        b_copy(k, 5).start()
        b_copy(k, 1).wait_recv()
        b_copy(k, 4).start()
        b_copy(k, 6).start()

    def diagonal_step(k):
        b_copy(k, 3).wait_recv()
        b_copy(k, 7).start()
        b_copy(k, 4).wait_recv()
        b_copy(k, 8).start()

    def partner_step(k, kinds):
        for kind in kinds:
            b_copy(k, kind).wait_recv()

    for k in range(1, n_e):
        z_copy(k).start()
        p_copy(k).start()
    own_step(0)

    ownp_copy.wait()
    for k in range(1, n_e):
        p_copy(k).wait_recv()
    for j in range(1, n_d):
        q_copy(j).start()
    own_p = pltpu.make_async_copy(pz, pall.at[d], local.at[3])
    own_p.start()
    sbuf[...] = jnp.zeros_like(sbuf)
    w_copy.wait()
    tile = 256 if depth % 256 == 0 else LANES

    @pl.loop(0, depth // tile)
    def _(i):
        at = pl.ds(pl.multiple_of(i * tile, tile), tile)
        wt[at, :] = wv[:, at].T

    own_step(1)
    side_step(0)
    own_p.wait()
    for j in range(1, n_d):
        q_copy(j).wait_recv()

    def back_step(k, gs):
        first, count = 2 * gs[0], 2 * len(gs)
        members = [pair(g) + c for g in gs for c in range(2)]
        r = jnp.concatenate([rows[k, m] for m in members], axis=0)
        back = jnp.dot(r, wt[...], preferred_element_type=F32)
        p = jnp.concatenate([as_column(pall[m, k, 0:1, :], cap) for m in members], axis=0)
        at = pl.ds(first, count)
        scaled[at] = (p * r.astype(F32)).astype(BF16).reshape(count, cap, depth)
        gbuf[k % 2, at] = (p * back).astype(BF16).reshape(count, cap, -1)
        h = hbuf[k % 2, at].reshape(count * cap, -1).astype(F32)
        slot = jnp.sum(h * back, axis=1, keepdims=True)
        for j, m in enumerate(members):
            sbuf[m, k : k + 1, :] = as_row(slot[j * cap : (j + 1) * cap], LANES)
        g_copy(k, gs).start()

    def weight_step(k, first, count, turned, add, final, start=0, stop=depth // width):
        @pl.loop(start, stop)
        def _(i):
            at = pl.ds(pl.multiple_of(i * width, width), width)
            part = jnp.dot(
                turned[:, 0 : count * cap],
                scaled[first : first + count, :, at].reshape(count * cap, width),
                preferred_element_type=F32,
            )
            if add:
                part = acc[:, at] + part
            if final:
                gdb[:, at] = part.astype(BF16)
                pltpu.make_async_copy(gdb.at[:, at], gd_ref.at[:, at], d_sem.at[i]).start()
            else:
                acc[:, at] = part

    columns = depth // width
    early, late = columns * 3 // 8, columns * 3 // 4
    for k in range(n_e):
        last = k == n_e - 1
        h_copy(k).wait()
        if k >= 2:
            g_copy(k - 2).wait()
        partner_step(k, (2, 5))
        back_step(k, (0, 1))
        if k == 0:
            diagonal_step(0)
        partner_step(k, (6,))
        if not last:
            ht[...] = hbuf[k % 2].reshape(n_d * cap, -1).T
            partner_step(k, (7, 8))
            back_step(k, (2, 3))
            side_step(k + 1)
            weight_step(k, 0, n_d, ht, k > 0, False, 0, early)
            if k + 2 < n_e:
                own_step(k + 2)
            weight_step(k, 0, n_d, ht, k > 0, False, early, late)
            diagonal_step(k + 1)
            weight_step(k, 0, n_d, ht, k > 0, False, late)
            if k + 2 < n_e:
                h_copy(k + 2).start()
        else:
            back_step(k, (2,))
            most = n_d - 2
            ht[:, 0 : most * cap] = hbuf[k % 2, 0:most].reshape(most * cap, -1).T
            ht_last[...] = hbuf[k % 2, most:n_d].reshape(2 * cap, -1).T
            weight_step(k, 0, most, ht, k > 0, False)
            partner_step(k, (7, 8))
            back_step(k, (3,))
            weight_step(k, most, 2, ht_last, True, True, 0, 1)
            for j in range(1, n_d):
                s_copy(j).start()
            weight_step(k, most, 2, ht_last, True, True, 1)

    total = sbuf[d]
    for j in range(1, n_d):
        s_copy(j).wait_recv()
        total = total + sall[j]
    tot[...] = total
    for k in range(1, n_e):
        t_copy(k).start()
    top, tokens = dest_ref.shape
    lanes = iota((LANES, tokens), 0)
    result = [jnp.zeros((1, tokens), F32) for _ in range(top)]
    for k in range(n_e):
        if k > 0:
            t_copy(k).wait_recv()
            row = tall[k][k : k + 1, :]
        else:
            row = total[0:1, :]
        column = as_column(row, LANES)
        base = flip(z, k) * LANES
        for t in range(top):
            hit = dest_ref[t : t + 1, :] == base + lanes
            result[t] = result[t] + jnp.sum(jnp.where(hit, column, 0.0), axis=0, keepdims=True)
    for t in range(top):
        gp_ref[t : t + 1, :] = result[t]

    for k in range(1, n_e):
        z_copy(k).wait_send()
        p_copy(k).wait_send()
        t_copy(k).wait_send()
    for j in range(1, n_d):
        q_copy(j).wait_send()
        s_copy(j).wait_send()
    for k in range(n_e):
        for kind in range(9):
            b_copy(k, kind).wait_send()
    for k in range(max(0, n_e - 2), n_e):
        g_copy(k).wait()

    @pl.loop(0, depth // width)
    def _(i):
        at = pl.ds(pl.multiple_of(i * width, width), width)
        pltpu.make_async_copy(gdb.at[:, at], gd_ref.at[:, at], d_sem.at[i]).wait()


def on_device(grad_out, probs, routes, hidden, w_down):
    n_e, n_d = lax.axis_size("expert"), lax.axis_size("dp")
    tokens, top = routes.shape
    cap = tokens * top * 5 // (4 * n_e)
    depth = grad_out.shape[1]
    units = hidden.shape[2]
    slots = n_d * cap
    vmem = pl.BlockSpec(memory_space=pltpu.VMEM)
    hbm = pl.BlockSpec(memory_space=pl.ANY)
    rows, p, dest = pl.pallas_call(
        functools.partial(pack_kernel, n_e, cap),
        out_shape=(
            jax.ShapeDtypeStruct((n_e, cap, depth), BF16),
            jax.ShapeDtypeStruct((n_e, SUB, LANES), F32),
            jax.ShapeDtypeStruct((top, tokens), jnp.int32),
        ),
        in_specs=[vmem] * 3,
        out_specs=(vmem, vmem, vmem),
        name="pack",
    )(grad_out, probs.T, routes.T)
    dma = pltpu.SemaphoreType.DMA
    chunks = max(1, depth // 256)
    gh, gd, gp = pl.pallas_call(
        functools.partial(main_kernel, n_e, n_d, cap),
        out_shape=(
            jax.ShapeDtypeStruct((n_d, n_e, cap, units), BF16),
            jax.ShapeDtypeStruct((units, depth), BF16),
            jax.ShapeDtypeStruct((top, tokens), F32),
        ),
        in_specs=[hbm, hbm, vmem, hbm, hbm],
        out_specs=(hbm, hbm, vmem),
        scratch_shapes=[
            pltpu.VMEM((n_e, n_d, cap, depth), BF16),
            pltpu.VMEM((units, depth), BF16),
            pltpu.VMEM((depth, units), BF16),
            pltpu.VMEM((2, n_d, cap, units), BF16),
            pltpu.VMEM((2, n_d, cap, units), BF16),
            pltpu.VMEM((units, slots), BF16),
            pltpu.VMEM((units, 2 * cap), BF16),
            pltpu.VMEM((n_d, cap, depth), BF16),
            pltpu.VMEM((units, depth), F32),
            pltpu.VMEM((units, depth), BF16),
            pltpu.VMEM((n_e, SUB, LANES), F32),
            pltpu.VMEM((n_d, n_e, SUB, LANES), F32),
            pltpu.VMEM((n_d, SUB, LANES), F32),
            pltpu.VMEM((n_d, SUB, LANES), F32),
            pltpu.VMEM((SUB, LANES), F32),
            pltpu.VMEM((n_e, SUB, LANES), F32),
            dma((n_e,)), dma((n_e,)),
            dma((n_e, 9)), dma((n_e, 9)),
            dma((n_e,)), dma((n_e,)),
            dma((n_d,)), dma((n_d,)),
            dma((n_d,)), dma((n_d,)),
            dma((n_e,)), dma((n_e,)),
            dma((4,)), dma((2, n_d // 2)), dma((2, n_d // 2)), dma((chunks,)),
        ],
        compiler_params=pltpu.CompilerParams(
            collective_id=0, has_side_effects=True, vmem_limit_bytes=62 * 1024 * 1024
        ),
        name="expert_back",
    )(rows, p, dest, hidden[0].reshape(n_d, n_e, cap, units), w_down[0])
    return gh.reshape(1, n_d * n_e * cap, units), gd[None], gp.T


def solution(mesh):
    in_specs = (
        P(("dp", "expert"), None),
        P(("dp", "expert"), None),
        P(("dp", "expert"), None),
        P("expert", None, "dp"),
        P("expert", "dp", None),
    )
    out_specs = (P("expert", None, "dp"), P("expert", "dp", None), P(("dp", "expert"), None))
    return jax.shard_map(
        on_device, mesh=mesh, in_specs=in_specs, out_specs=out_specs, check_vma=False
    )
```
